256 devices in a mesh: ha: 32 (over z, x_hi, core), wa: 8 (over y, x_lo).
Axes of the slice: x: 4 (x_hi: 2, x_lo: 2; x = x_hi * 2 + x_lo), y: 4, z: 8, core: 2. Of those that a mesh axis runs over, the one named last changes fastest.
Arguments:
- queries: bfloat16 [512, 512, 384], P('ha', 'wa'), may hold values from -200 to 200
- key_tokens: bfloat16 [512, 512, 384], P('ha', 'wa'), may hold values from -6 to 6
- value_tokens: bfloat16 [512, 512, 384], P('ha', 'wa'), may hold values from -6 to 6
- out_grad: bfloat16 [512, 512, 384], P('ha', 'wa'), may hold values from -96 to 96
- key_kernel: bfloat16 [3, 3, 384], replicated, may hold values from -2 to 2
- value_kernel: bfloat16 [3, 3, 384], replicated, may hold values from -2 to 2
- height_table: bfloat16 [1023, 96], replicated, may hold values from -0.8984375 to 0.8984375
- width_table: bfloat16 [1023, 96], replicated, may hold values from -0.8984375 to 0.8984375
Outputs:
- query_grad: bfloat16 [512, 512, 384], P('ha', 'wa')
- key_grad: bfloat16 [512, 512, 384], P('ha', 'wa')
- value_grad: bfloat16 [512, 512, 384], P('ha', 'wa')
- height_grad: float32 [1023, 96], replicated
- width_grad: float32 [1023, 96], replicated
The draws below stay inside these ranges and needn't reach their ends.
All inputs are finite; a program needn't handle non-finite values.
Results may differ from the reference program's by a relative error of at most 0.02.
The reference program's roundings to bfloat16 on the way (of `key_pooled`, `height_rows`, `probs_low` and `grad_low`) count: a program that leaves them out, or rounds other values in their place, can miss the bound.
Values may be sent and summed in bfloat16 or wider, within the bound.
No kernel may reach another device: no remote copies, remote signals or barrier semaphores. Data moves between devices by JAX's collectives and lax.ppermute only.
A program may use at most 128 MiB of HBM per device.

```python
import jax
import jax.numpy as jnp
from jax import lax

HEADS = 4
HD = 96
C = 384
KS = 3
STRIDE = 16
RH = 16
H = 512
W = 512
PH = 32
PW = 32
KEYS = 1024
TH = 1023
TW = 1023
N_HA = 32


def draw_queries(key, part):
    first_key = jax.random.fold_in(key, 0)
    values = jnp.clip(jax.random.normal(first_key, (H, W, HEADS * HD), jnp.float32), -5.0, 5.0)
    return values.astype(jnp.bfloat16)


def steps_of(rng, dims, shards, least, largest):
    def one(axis_at, blocks):
        draws = jax.random.uniform(jax.random.fold_in(jax.random.fold_in(rng, 6), axis_at), (blocks,), jnp.float32, least / len(shards), largest / len(shards))
        return jnp.repeat(jnp.exp(draws), dims[axis_at] // blocks).reshape((-1,) + (1,) * (len(dims) - axis_at - 1))

    loudness = one(*shards[0])
    for cut in shards[1:]:
        loudness = loudness * one(*cut)
    return loudness


def normal_values(own_key, shape, spread, reach, cuts=(), kind=jnp.bfloat16):
    loudness = steps_of(own_key, shape, cuts, -0.22, 0.18) if cuts else 1.0
    entries = jax.random.normal(own_key, shape, jnp.float32) * spread * loudness
    return jnp.minimum(jnp.maximum(entries, -reach), reach).astype(kind)


def setup_inputs(seed: int = 0) -> dict:
    seeds = jax.random.split(jax.random.key(seed), 9)
    return {
        "queries": draw_queries(jax.random.fold_in(seeds[8], 71), 0),
        "key_tokens": normal_values(seeds[1], (H, W, C), 1.0, 6.0, ((0, 32), (1, 8))),
        "value_tokens": normal_values(seeds[2], (H, W, C), 1.0, 6.0, ((0, 32), (1, 8))),
        "out_grad": normal_values(seeds[3], (H, W, C), 16.0, 96.0, ((0, 32), (1, 8))),
        "key_kernel": normal_values(seeds[4], (KS, KS, C), (KS * KS) ** -0.5, 2.0),
        "value_kernel": normal_values(seeds[5], (KS, KS, C), (KS * KS) ** -0.5, 2.0),
        "height_table": normal_values(seeds[6], (TH, HD), 0.15, 0.8984375),
        "width_table": normal_values(seeds[7], (TW, HD), 0.15, 0.8984375),
    }


highest = lax.Precision.HIGHEST

def pool_global(tokens, kernel):
    halfwidth = KS // 2
    pooled = lax.conv_general_dilated(tokens.astype(jnp.float32)[None], kernel.astype(jnp.float32)[:, :, None, :], (STRIDE, STRIDE), ((halfwidth, halfwidth), (halfwidth, halfwidth)), dimension_numbers=('NHWC', 'HWIO', 'NHWC'), feature_group_count=tokens.shape[-1], precision=highest)
    return pooled[0]

def rounded(values):
    return lax.optimization_barrier(values.astype(jnp.bfloat16)).astype(jnp.float32)

def reference(queries, key_tokens, value_tokens, out_grad, key_kernel, value_kernel, height_table, width_table):
    score_scale = HD ** (-0.5)
    key_pooled = rounded(pool_global(key_tokens, key_kernel)).reshape(KEYS, HEADS, HD)
    value_pooled = rounded(pool_global(value_tokens, value_kernel)).reshape(KEYS, HEADS, HD)
    height_dist = (jnp.arange(H)[:, None] - STRIDE * jnp.arange(PH)[None, :] + (PH - 1) * STRIDE).astype(jnp.int32)
    width_dist = (jnp.arange(W)[:, None] - STRIDE * jnp.arange(PW)[None, :] + (PW - 1) * STRIDE).astype(jnp.int32)
    height_rows = height_table[height_dist].astype(jnp.float32)
    width_rows = width_table[width_dist].astype(jnp.float32)

    def block_step(totals, block_index):
        key_acc, value_acc, height_acc, width_acc = totals
        first_row = (block_index * RH).astype(jnp.int32)
        query_block = lax.dynamic_slice_in_dim(queries, first_row, RH, 0).astype(jnp.float32).reshape(RH, W, HEADS, HD)
        grad_block = lax.dynamic_slice_in_dim(out_grad, first_row, RH, 0).astype(jnp.float32).reshape(RH, W, HEADS, HD)
        height_block = lax.dynamic_slice_in_dim(height_rows, first_row, RH, 0)
        dist_block = lax.dynamic_slice_in_dim(height_dist, first_row, RH, 0)
        rel_height = jnp.einsum('rwnd,rkd->rwnk', query_block, height_block, precision=highest)
        rel_width = jnp.einsum('rwnd,wkd->rwnk', query_block, width_rows, precision=highest)
        score_bias = (rel_height[..., :, None] + rel_width[..., None, :]).reshape(RH * W, HEADS, KEYS)
        query_flat = query_block.reshape(RH * W, HEADS, HD)
        grad_flat = grad_block.reshape(RH * W, HEADS, HD)
        scores = score_scale * jnp.einsum('tnd,knd->tnk', query_flat, key_pooled, precision=highest) + score_bias
        scores = scores - lax.optimization_barrier(jnp.max(scores, axis=-1, keepdims=True))
        weights = jnp.exp(scores)
        attention = weights / lax.optimization_barrier(jnp.sum(weights, axis=-1, keepdims=True))
        probs_low = rounded(attention)
        attended = jnp.einsum('tnk,knd->tnd', probs_low, value_pooled, precision=highest)
        grad_probs = jnp.einsum('tnd,knd->tnk', grad_flat, value_pooled, precision=highest)
        row_delta = lax.optimization_barrier(jnp.sum(grad_flat * attended, axis=-1, keepdims=True))
        grad_scores = attention * (grad_probs - row_delta)
        grad_low = rounded(grad_scores)
        query_attn = score_scale * jnp.einsum('tnk,knd->tnd', grad_low, key_pooled, precision=highest)
        key_acc = key_acc + score_scale * jnp.einsum('tnk,tnd->knd', grad_low, query_flat, precision=highest)
        value_acc = value_acc + jnp.einsum('tnk,tnd->knd', probs_low, grad_flat, precision=highest)
        score_grid = grad_scores.reshape(RH, W, HEADS, PH, PW)
        grad_height = lax.optimization_barrier(jnp.sum(score_grid, axis=-1))
        grad_width = lax.optimization_barrier(jnp.sum(score_grid, axis=-2))
        query_rel = jnp.einsum('rwnk,rkd->rwnd', grad_height, height_block, precision=highest) + jnp.einsum('rwnk,wkd->rwnd', grad_width, width_rows, precision=highest)
        query_grad = (query_attn.reshape(RH, W, HEADS, HD) + query_rel).reshape(RH, W, HEADS * HD).astype(jnp.bfloat16)
        height_acc = height_acc.at[dist_block].add(jnp.einsum('rwnk,rwnd->rkd', grad_height, query_block, precision=highest))
        width_acc = width_acc.at[width_dist].add(jnp.einsum('rwnk,rwnd->wkd', grad_width, query_block, precision=highest))
        return ((key_acc, value_acc, height_acc, width_acc), query_grad)
    initial = (jnp.zeros((KEYS, HEADS, HD), jnp.float32), jnp.zeros((KEYS, HEADS, HD), jnp.float32), jnp.zeros((TH, HD), jnp.float32), jnp.zeros((TW, HD), jnp.float32))
    totals, blocks = lax.scan(block_step, initial, jnp.arange(N_HA))
    key_acc, value_acc, height_acc, width_acc = totals
    query_grad = blocks.reshape(H, W, HEADS * HD)
    _, key_back = jax.vjp(lambda tokens: pool_global(tokens, key_kernel), key_tokens.astype(jnp.float32))
    key_grad = key_back(key_acc.reshape(PH, PW, HEADS * HD))[0].astype(jnp.bfloat16)
    _, value_back = jax.vjp(lambda tokens: pool_global(tokens, value_kernel), value_tokens.astype(jnp.float32))
    value_grad = value_back(value_acc.reshape(PH, PW, HEADS * HD))[0].astype(jnp.bfloat16)
    return (query_grad, key_grad, value_grad, height_acc, width_acc)
```

```python
import math

import jax
import jax.numpy as jnp
from jax import lax
from jax.experimental import pallas as pl
from jax.experimental.pallas import tpu as pltpu
from jax.sharding import PartitionSpec as P

HEADS = 4
HD = 96
C = HEADS * HD
STRIDE = 16
F32 = jnp.float32
BF16 = jnp.bfloat16
SCALE = HD ** (-0.5)
ROOT = HD ** 0.5
EXPONENT = SCALE / math.log(2.0)
WIN = 256
TB = 256


def window_start(n):
    return 128 * (n // 2)


def taps(kernel, row):
    return [kernel[row, i].astype(F32) for i in range(3)]


def cell_sums(before, first, second):
    zero = jnp.zeros((1, C), F32)
    return jnp.concatenate([first + second, zero], 0) + jnp.concatenate([zero, before], 0)


def pool_partial(tokens, kernel):
    def pieces(row):
        cells = tokens[row].astype(F32).reshape(-1, STRIDE, C)
        return cells[:, STRIDE - 1], cells[:, 0], cells[:, 1]

    def weighted(row, kernel_row):
        left, mid, right = taps(kernel, kernel_row)
        before, first, second = pieces(row)
        return before * left, first * mid, second * right

    own = [a + b for a, b in zip(weighted(0, 1), weighted(1, 2))]
    return jnp.stack([cell_sums(*own), cell_sums(*weighted(STRIDE - 1, 0))])


def spread_rows(cot, kernel, kernel_row):
    left, mid, right = taps(kernel, kernel_row)
    cells = cot.shape[0] - 1
    zeros = jnp.zeros((cells, STRIDE - 3, C), F32)
    row = jnp.concatenate(
        [
            (cot[:cells] * mid)[:, None],
            (cot[:cells] * right)[:, None],
            zeros,
            (cot[1:] * left)[:, None],
        ],
        1,
    )
    return row.reshape(cells * STRIDE, C)


def spread(cot, kernel):
    top = spread_rows(cot[0], kernel, 1)
    second = spread_rows(cot[0], kernel, 2)
    last = spread_rows(cot[1], kernel, 0)
    zeros = jnp.zeros((STRIDE - 3,) + top.shape, BF16)
    return jnp.concatenate(
        [top.astype(BF16)[None], second.astype(BF16)[None], zeros, last.astype(BF16)[None]], 0
    )


def shift(block, axis, distance):
    size = lax.axis_size(axis)
    return lax.ppermute(
        block, axis, [(i, i + distance) for i in range(size) if 0 <= i + distance < size]
    )


def shift_both(block, distance):
    rows, cols = lax.axis_size("ha"), lax.axis_size("wa")
    route = [
        (i * cols + j, (i + distance) * cols + j + distance)
        for i in range(rows)
        for j in range(cols)
        if 0 <= i + distance < rows and 0 <= j + distance < cols
    ]
    return lax.ppermute(block, ("ha", "wa"), route)


def to_all(block, axis):
    copies = jnp.broadcast_to(block[None], (lax.axis_size(axis),) + block.shape)
    return lax.all_to_all(copies, axis, 0, 0, tiled=False)


def exchange(blocks, axis):
    return lax.all_to_all(blocks, axis, 0, 0, tiled=False)


def dot(a, b):
    return jnp.dot(a, b, preferred_element_type=F32)


def attention_kernel(
    kv_ref, qt_ref, gt_ref, q_ref, g_ref, hexp_ref, wexp_ref,
    sums_ref, dq_ref, rel_ref,
    k_s, v_s, kt_s, vt_s, e_s, p_s, d_s, ks_s, vs_s, gh_s, gw_s,
):
    n = pl.program_id(0)
    keys = k_s.shape[0]
    tokens = q_ref.shape[1]
    groups = keys // 128

    @pl.when(n == 0)
    def _():
        half = kv_ref.shape[0] // 2
        low = lax.broadcasted_iota(jnp.int32, (half, 8, C), 1) < 4
        pair = kv_ref[...].astype(F32).reshape(half, 2, 8, C)
        a, b = pair[:, 0], pair[:, 1]
        k = jnp.where(low, a, pltpu.roll(b, 4, 1)).reshape(keys, C)
        v = jnp.where(low, pltpu.roll(a, 4, 1), b).reshape(keys, C)
        k_s[...] = k.astype(BF16)
        v_s[...] = v.astype(BF16)
        kt_s[...] = k.T.astype(BF16)
        vt_s[...] = v.T.astype(BF16)
        ks_s[...] = jnp.zeros_like(ks_s)
        vs_s[...] = jnp.zeros_like(vs_s)

    win = pl.multiple_of(128 * (n // 2), 128)
    own = pl.multiple_of(HD * n - 128 * (n // 2), 32)
    rows = pl.multiple_of(HD * n, 32)
    kwin = pl.ds(win, WIN)

    for tb in range(tokens // TB):
        cols = pl.ds(tb * TB, TB)
        qt = qt_ref[0, :, cols]
        gt = gt_ref[0, :, cols]
        hexp = hexp_ref[0, :, cols]
        top = jnp.full((8, TB), -jnp.inf, F32)
        for w in range(groups):
            part = pl.ds(w * 128, 128)
            s = dot(k_s[part, kwin], qt)
            bias = wexp_ref[0, pl.ds(w * 8, 8), cols]
            s = ((s + hexp).reshape(16, 8, TB) + bias[None])
            top = jnp.maximum(top, jnp.max(s, axis=0))
            e_s[part, :] = s.reshape(128, TB)
        top = jnp.max(top, axis=0, keepdims=True)
        total = jnp.zeros((8, TB), F32)
        for w in range(groups):
            part = pl.ds(w * 128, 128)
            e = jnp.exp2((e_s[part, :] - top) * EXPONENT)
            total = total + jnp.sum(e.reshape(16, 8, TB), axis=0)
            e_s[part, :] = e
        inverse = 1.0 / jnp.sum(total, axis=0, keepdims=True)
        for w in range(groups):
            part = pl.ds(w * 128, 128)
            p = e_s[part, :] * inverse
            e_s[part, :] = p
            p_s[part, cols] = p.astype(BF16)
        attended = dot(vt_s[pl.ds(rows, HD), :], p_s[:, cols])
        delta = jnp.sum(
            attended * gt_ref[0, pl.ds(own, HD), cols].astype(F32), axis=0, keepdims=True
        )
        height = jnp.zeros((128, TB), F32)
        for w in range(groups):
            part = pl.ds(w * 128, 128)
            d = e_s[part, :] * (dot(v_s[part, kwin], gt) - delta)
            d_s[part, cols] = d.astype(BF16)
            height = height + d
            width = jnp.sum(d.reshape(16, 8, TB), axis=0)
            for i in range(TB // 128):
                gw_s[i, pl.ds(w * 8, 8), :] = width[:, i * 128 : (i + 1) * 128]
        for i in range(TB // 128):
            lanes = pl.ds(tb * TB + i * 128, 128)
            gh_s[i] = height[:, i * 128 : (i + 1) * 128]
            sum_h = gh_s[i, pl.ds(0, 32, stride=4), :]
            for c in range(1, 4):
                sum_h = sum_h + gh_s[i, pl.ds(c, 32, stride=4), :]
            rel_ref[0, pl.ds(0, 32), lanes] = sum_h
            for c in range(4):
                rel_ref[0, pl.ds(32 + 8 * c, 8), lanes] = (
                    gw_s[i, pl.ds(c, groups, stride=8), :] + gw_s[i, pl.ds(c + 4, groups, stride=8), :]
                )
        dq_ref[0, :, cols] = dot(kt_s[pl.ds(rows, HD), :], d_s[:, cols]) * SCALE

    ks_s[:, kwin] += dot(d_s[...], q_ref[0])
    vs_s[:, kwin] += dot(p_s[...], g_ref[0])

    @pl.when(n == pl.num_programs(0) - 1)
    def _():
        half = keys // 8
        low = lax.broadcasted_iota(jnp.int32, (half, 8, C), 1) < 4
        k = ks_s[...].reshape(half, 8, C) * SCALE
        v = vs_s[...].reshape(half, 8, C)
        a = jnp.where(low, k, pltpu.roll(v, 4, 1))
        b = jnp.where(low, pltpu.roll(k, 4, 1), v)
        sums_ref[...] = jnp.stack([a, b], 1).reshape(2 * half, 8, C).astype(BF16)


def attention(kv, qt, gt, q, g, hexp, wexp):
    tokens = q.shape[1]
    keys = kv.shape[0] * 4
    whole = lambda shape: pl.BlockSpec(shape, lambda n: (0,) * len(shape))
    head = lambda shape: pl.BlockSpec((1,) + shape, lambda n: (n, 0, 0))
    return pl.pallas_call(
        attention_kernel,
        grid=(HEADS,),
        in_specs=[
            whole(kv.shape),
            head((WIN, tokens)),
            head((WIN, tokens)),
            head((tokens, WIN)),
            head((tokens, WIN)),
            head((128, tokens)),
            head((64, tokens)),
        ],
        out_specs=[whole(kv.shape), head((HD, tokens)), head((64, tokens))],
        out_shape=[
            jax.ShapeDtypeStruct(kv.shape, BF16),
            jax.ShapeDtypeStruct((HEADS, HD, tokens), F32),
            jax.ShapeDtypeStruct((HEADS, 64, tokens), F32),
        ],
        scratch_shapes=[
            pltpu.VMEM((keys, C), BF16),
            pltpu.VMEM((keys, C), BF16),
            pltpu.VMEM((C, keys), BF16),
            pltpu.VMEM((C, keys), BF16),
            pltpu.VMEM((keys, TB), F32),
            pltpu.VMEM((keys, tokens), BF16),
            pltpu.VMEM((keys, tokens), BF16),
            pltpu.VMEM((keys, C), F32),
            pltpu.VMEM((keys, C), F32),
            pltpu.VMEM((TB // 128, 128, 128), F32),
            pltpu.VMEM((TB // 128, 64, 128), F32),
        ],
        compiler_params=pltpu.CompilerParams(
            dimension_semantics=("arbitrary",), vmem_limit_bytes=60 * 1024 * 1024
        ),
        cost_estimate=pl.CostEstimate(
            flops=12 * keys * tokens * C, bytes_accessed=20 * 1024 * 1024,
            transcendentals=keys * tokens * HEADS,
        ),
        name="attention",
    )(kv, qt, gt, q, g, hexp, wexp)


def windows(x):
    out = []
    for n in range(HEADS):
        left = HD * n - window_start(n)
        out.append(jnp.pad(x[:, HD * n : HD * (n + 1)], ((0, 0), (left, WIN - left - HD))))
    return jnp.stack(out)


def windows_t(x):
    xt = x.T
    out = []
    for n in range(HEADS):
        left = HD * n - window_start(n)
        out.append(jnp.pad(xt[HD * n : HD * (n + 1)], ((left, WIN - left - HD), (0, 0))))
    return jnp.stack(out)


def split(x):
    high = x.astype(BF16)
    return high, (x - high.astype(F32)).astype(BF16)


def einsum2(spec, x, y):
    high, low = split(x)
    return jnp.einsum(spec, high, y, preferred_element_type=F32) + jnp.einsum(
        spec, low, y, preferred_element_type=F32
    )


def on_device(
    queries, key_tokens, value_tokens, out_grad, key_kernel, value_kernel, height_table, width_table
):
    own_rows, own_cols, _ = queries.shape
    rows_n, cols_n = lax.axis_size("ha"), lax.axis_size("wa")
    tokens = own_rows * own_cols
    cells = own_cols // STRIDE
    key_rows, key_cols = rows_n, cols_n * cells
    ha, wa = lax.axis_index("ha"), lax.axis_index("wa")

    part = jnp.stack([pool_partial(key_tokens, key_kernel), pool_partial(value_tokens, value_kernel)])
    above = shift(part[:, 1, :cells], "ha", 1)
    left = shift(part[:, 0, cells:], "wa", 1)
    corner = shift_both(part[:, 1, cells:], 1)
    own = part[:, 0, :cells] + above
    own = jnp.concatenate([own[:, :1] + (left + corner), own[:, 1:]], 1)
    pooled = own.astype(BF16).reshape(2 * cells, C)
    gathered = to_all(to_all(pooled, "ha"), "wa").reshape(cols_n * rows_n, 2 * cells, C)

    q_flat = queries.reshape(tokens, C)
    g_flat = out_grad.reshape(tokens, C)
    height_rows = jnp.stack(
        [
            lax.dynamic_slice_in_dim(height_table, STRIDE * (ha + key_rows - 1 - k), own_rows, 0)
            for k in range(key_rows)
        ],
        1,
    )
    width_rows = jnp.stack(
        [
            lax.dynamic_slice_in_dim(
                width_table, own_cols * wa + STRIDE * (key_cols - 1 - k), own_cols, 0
            )
            for k in range(key_cols)
        ],
        1,
    )
    q_heads = queries.reshape(own_rows, own_cols, HEADS, HD)
    height_exp = jnp.repeat(height_rows, cells, axis=1)
    width_exp = jnp.broadcast_to(
        width_rows.reshape(own_cols, cols_n, 1, cells, HD), (own_cols, cols_n, 2, cells, HD)
    ).reshape(own_cols, 2 * key_cols, HD)
    hexp = jnp.einsum("rwnd,rkd->nkrw", q_heads, height_exp, preferred_element_type=F32) * ROOT
    wexp = jnp.einsum("rwnd,wkd->nkrw", q_heads, width_exp, preferred_element_type=F32) * ROOT
    hexp = hexp.reshape(HEADS, cells * key_rows, tokens)
    wexp = wexp.reshape(HEADS, 2 * key_cols, tokens)

    sums, dq, rel = attention(
        gathered, windows_t(q_flat), windows_t(g_flat), windows(q_flat), windows(g_flat), hexp, wexp
    )

    sums = exchange(sums.reshape(cols_n, rows_n, 2 * cells, C), "wa")

    grad_h = rel[:, :key_rows].reshape(HEADS, key_rows, own_rows, own_cols)
    grad_w = rel[:, key_rows:].reshape(HEADS, cells, cols_n, own_rows, own_cols)
    grad_w = grad_w.transpose(0, 2, 1, 3, 4).reshape(HEADS, key_cols, own_rows, own_cols)
    h_local = einsum2("nkrw,rwnd->krd", grad_h, q_heads)
    w_local = einsum2("nkrw,rwnd->kwd", grad_w, q_heads)
    h_window = h_local[::-1].reshape(key_rows * own_rows, HD)
    w_blocks = w_local[::-1].reshape(key_cols, cells, STRIDE, HD)
    w_window = sum(
        jnp.pad(w_blocks[:, a], ((a, cells - 1 - a), (0, 0), (0, 0))) for a in range(cells)
    ).reshape((key_cols + cells - 1) * STRIDE, HD)
    size = 1024
    table = jnp.zeros((2, size, HD), BF16)
    table = lax.dynamic_update_slice(table, h_window.astype(BF16)[None], (0, own_rows * ha, 0))
    table = lax.dynamic_update_slice(table, w_window.astype(BF16)[None], (1, own_cols * wa, 0))
    chunk = size // rows_n
    table = table.reshape(2, rows_n, chunk, HD).transpose(1, 0, 2, 3).reshape(rows_n, 2 * chunk, HD)
    table = jnp.sum(exchange(table, "ha").astype(F32), 0).astype(BF16)

    sums = jnp.sum(sums.astype(F32), 0).astype(BF16)
    sums = jnp.sum(exchange(sums, "ha").astype(F32), 0).reshape(2, cells, C)
    table = jnp.sum(to_all(table, "wa").astype(F32), 0).astype(BF16)
    table = to_all(table, "ha").astype(F32)
    table = table.reshape(rows_n, 2, chunk, HD).transpose(1, 0, 2, 3).reshape(2, size, HD)
    height_grad = table[0, : height_table.shape[0]]
    width_grad = table[1, : width_table.shape[0]]

    right = shift(sums[:, :1], "wa", -1)
    below = shift(sums, "ha", -1)
    corner = shift_both(sums[:, :1], -1)
    cot = jnp.stack(
        [jnp.concatenate([sums, right], 1), jnp.concatenate([below, corner], 1)], 1
    )
    key_grad = spread(cot[0], key_kernel)
    value_grad = spread(cot[1], value_kernel)

    query_rel = einsum2("nkrw,rkd->ndrw", grad_h, height_rows) + einsum2(
        "nkrw,wkd->ndrw", grad_w, width_rows
    )
    query_grad = dq.reshape(C, tokens) + query_rel.reshape(C, tokens)
    query_grad = query_grad.T.astype(BF16).reshape(own_rows, own_cols, C)
    return (query_grad, key_grad, value_grad, height_grad, width_grad)


def solution(mesh):
    placed = P("ha", "wa", None)
    return jax.shard_map(
        on_device,
        mesh=mesh,
        in_specs=(placed,) * 4 + (P(),) * 4,
        out_specs=(placed, placed, placed, P(), P()),
        check_vma=False,
    )
```

```python
import math

import jax
import jax.numpy as jnp
from jax import lax
from jax.experimental import pallas as pl
from jax.experimental.pallas import tpu as pltpu
from jax.sharding import PartitionSpec as P

HEADS = 4
HD = 96
C = HEADS * HD
STRIDE = 16
F32 = jnp.float32
BF16 = jnp.bfloat16
SCALE = HD ** (-0.5)
ROOT = HD ** 0.5
EXPONENT = SCALE / math.log(2.0)
WIN = 256
TB = 256


def window_start(n):
    return 128 * (n // 2)


def taps(kernel, row):
    return [kernel[row, i].astype(F32) for i in range(3)]


def cell_sums(before, first, second):
    zero = jnp.zeros((1, C), F32)
    return jnp.concatenate([first + second, zero], 0) + jnp.concatenate([zero, before], 0)


def pool_partial(tokens, kernel):
    def pieces(row):
        cells = tokens[row].astype(F32).reshape(-1, STRIDE, C)
        return cells[:, STRIDE - 1], cells[:, 0], cells[:, 1]

    def weighted(row, kernel_row):
        left, mid, right = taps(kernel, kernel_row)
        before, first, second = pieces(row)
        return before * left, first * mid, second * right

    own = [a + b for a, b in zip(weighted(0, 1), weighted(1, 2))]
    return jnp.stack([cell_sums(*own), cell_sums(*weighted(STRIDE - 1, 0))])


def spread_rows(cot, kernel, kernel_row):
    left, mid, right = taps(kernel, kernel_row)
    cells = cot.shape[0] - 1
    zeros = jnp.zeros((cells, STRIDE - 3, C), F32)
    row = jnp.concatenate(
        [
            (cot[:cells] * mid)[:, None],
            (cot[:cells] * right)[:, None],
            zeros,
            (cot[1:] * left)[:, None],
        ],
        1,
    )
    return row.reshape(cells * STRIDE, C)


def spread(cot, kernel):
    top = spread_rows(cot[0], kernel, 1)
    second = spread_rows(cot[0], kernel, 2)
    last = spread_rows(cot[1], kernel, 0)
    zeros = jnp.zeros((STRIDE - 3,) + top.shape, BF16)
    return jnp.concatenate(
        [top.astype(BF16)[None], second.astype(BF16)[None], zeros, last.astype(BF16)[None]], 0
    )


def shift(block, axis, distance):
    size = lax.axis_size(axis)
    return lax.ppermute(
        block, axis, [(i, i + distance) for i in range(size) if 0 <= i + distance < size]
    )


def shift_both(block, distance):
    rows, cols = lax.axis_size("ha"), lax.axis_size("wa")
    route = [
        (i * cols + j, (i + distance) * cols + j + distance)
        for i in range(rows)
        for j in range(cols)
        if 0 <= i + distance < rows and 0 <= j + distance < cols
    ]
    return lax.ppermute(block, ("ha", "wa"), route)


def swap(block):
    return lax.ppermute(block, "ha", [(i, i ^ 1) for i in range(lax.axis_size("ha"))])


def to_all(block, axis):
    copies = jnp.broadcast_to(block[None], (lax.axis_size(axis),) + block.shape)
    return lax.all_to_all(copies, axis, 0, 0, tiled=False)


def exchange(blocks, axis):
    return lax.all_to_all(blocks, axis, 0, 0, tiled=False)


def dot(a, b):
    return jnp.dot(a, b, preferred_element_type=F32)


def token_masks(width, first):
    at = lax.broadcasted_iota(jnp.int32, (STRIDE, width), 1) + first
    entry = lax.broadcasted_iota(jnp.int32, (STRIDE, width), 0)
    return at // STRIDE == entry, at % STRIDE == entry


def prep_kernel(q_ref, g_ref, th_ref, tw_ref, qt_ref, gt_ref, hexp_ref, wexp_ref):
    jb = pl.program_id(0)
    row_mask, col_mask = token_masks(TB, 0)
    sub = lax.broadcasted_iota(jnp.int32, (8, TB), 0) % 4
    low = lax.broadcasted_iota(jnp.int32, (8, TB), 0) < 4
    qt = q_ref[...].astype(F32).reshape(TB, C).T.astype(BF16)
    gt = g_ref[...].astype(F32).reshape(TB, C).T.astype(BF16)
    shifted = pl.ds(pl.multiple_of(STRIDE * jb, STRIDE), th_ref.shape[0])
    qt_ref[...] = jnp.zeros_like(qt_ref)
    gt_ref[...] = jnp.zeros_like(gt_ref)
    for n in range(HEADS):
        left = HD * n - window_start(n)
        q_n = qt[HD * n : HD * (n + 1)]
        qt_ref[n, pl.ds(left, HD), :] = q_n
        gt_ref[n, pl.ds(left, HD), :] = gt[HD * n : HD * (n + 1)]

        def picked(table, mask):
            full = dot(table, q_n).reshape(-1, STRIDE, TB)
            full = jnp.where(mask[None], full, 0.0)
            return jnp.sum(full, axis=1, keepdims=True) * ROOT

        rel = picked(th_ref[...], row_mask)
        count = rel.shape[0]
        spread_to = lambda x: jnp.broadcast_to(x, (8, TB))
        for r in range(count // 2):
            hexp_ref[n, pl.ds(8 * r, 8), :] = jnp.where(
                low, spread_to(rel[count - 1 - 2 * r]), spread_to(rel[count - 2 - 2 * r])
            )
        rel = picked(tw_ref[shifted, :], col_mask)
        for w in range(count // 4):
            last = count - 1 - 4 * w
            value = spread_to(rel[last])
            for c in range(1, 4):
                value = jnp.where(sub == c, spread_to(rel[last - c]), value)
            wexp_ref[n, pl.ds(8 * w, 8), :] = value


def prepare(queries, out_grad, th, tw):
    rows, cols, _ = queries.shape
    tokens = rows * cols
    block = pl.BlockSpec((rows, STRIDE, C), lambda j: (0, j, 0))
    whole = lambda x: pl.BlockSpec(x.shape, lambda j: (0, 0))
    out = lambda n: pl.BlockSpec((HEADS, n, TB), lambda j: (0, 0, j))
    return pl.pallas_call(
        prep_kernel,
        grid=(tokens // TB,),
        in_specs=[block, block, whole(th), whole(tw)],
        out_specs=[out(WIN), out(WIN), out(128), out(64)],
        out_shape=[
            jax.ShapeDtypeStruct((HEADS, WIN, tokens), BF16),
            jax.ShapeDtypeStruct((HEADS, WIN, tokens), BF16),
            jax.ShapeDtypeStruct((HEADS, 128, tokens), F32),
            jax.ShapeDtypeStruct((HEADS, 64, tokens), F32),
        ],
        cost_estimate=pl.CostEstimate(
            flops=4 * 1024 * tokens * C, bytes_accessed=10 * 1024 * 1024, transcendentals=0
        ),
        name="prepare",
    )(queries, out_grad, th, tw)


def attention_kernel(
    at_ref, mine_ref, other_ref, qt_ref, gt_ref, q_ref, g_ref, hexp_ref, wexp_ref, tht_ref, twt_ref,
    keep_ref, send_ref, dq_ref,
    k_s, v_s, kt_s, vt_s, e_s, p_s, d_s, ks_s, vs_s, gh_s, gw_s, a_s, qz_s, gz_s, th_s, tw_s,
):
    n = pl.program_id(0)
    keys = k_s.shape[0]
    tokens = qt_ref.shape[2]
    groups = keys // 128
    span = tht_ref.shape[1]

    @pl.when(n == 0)
    def _():
        for parity, (k_ref, v_ref) in enumerate(
            ((mine_ref, other_ref), (other_ref, mine_ref))
        ):

            @pl.when(at_ref[2] == parity)
            def _(k_ref=k_ref, v_ref=v_ref):
                k_s[...] = k_ref[...]
                v_s[...] = v_ref[...]

        kt_s[...] = k_s[...].astype(F32).T.astype(BF16)
        vt_s[...] = v_s[...].astype(F32).T.astype(BF16)
        for ref in (ks_s, vs_s, th_s, tw_s):
            ref[...] = jnp.zeros_like(ref)

    win = pl.multiple_of(128 * (n // 2), 128)
    own = pl.multiple_of(HD * n - 128 * (n // 2), 32)
    rows = pl.multiple_of(HD * n, 32)
    kwin = pl.ds(win, WIN)
    lane = lax.broadcasted_iota(jnp.int32, (1, WIN), 1)
    lanes_on = ((lane >= own) & (lane < own + HD)).astype(F32).astype(BF16)

    for tb in range(tokens // TB):
        cols = pl.ds(tb * TB, TB)
        tile = (slice(None), pl.ds(tb * STRIDE, STRIDE), kwin)
        qz_s[cols, :] = q_ref[tile].reshape(TB, WIN) * lanes_on
        gz_s[cols, :] = g_ref[tile].reshape(TB, WIN) * lanes_on
        qt = qt_ref[0, :, cols]
        gt = gt_ref[0, :, cols]
        hexp = hexp_ref[0, :, cols]
        top = jnp.full((8, TB), -jnp.inf, F32)
        for w in range(groups):
            part = pl.ds(w * 128, 128)
            s = dot(k_s[part, kwin], qt)
            bias = wexp_ref[0, pl.ds(w * 8, 8), cols]
            s = (s + hexp).reshape(16, 8, TB) + bias[None]
            top = jnp.maximum(top, jnp.max(s, axis=0))
            e_s[part, :] = s.reshape(128, TB)
        top = jnp.max(top, axis=0, keepdims=True)
        total = jnp.zeros((8, TB), F32)
        for w in range(groups):
            part = pl.ds(w * 128, 128)
            e = jnp.exp2((e_s[part, :] - top) * EXPONENT)
            total = total + jnp.sum(e.reshape(16, 8, TB), axis=0)
            e_s[part, :] = e
        inverse = 1.0 / jnp.sum(total, axis=0, keepdims=True)
        for w in range(groups):
            part = pl.ds(w * 128, 128)
            p = e_s[part, :] * inverse
            e_s[part, :] = p
            p_s[part, cols] = p.astype(BF16)
        attended = dot(vt_s[pl.ds(rows, HD), :], p_s[:, cols])
        delta = jnp.sum(
            attended * gt_ref[0, pl.ds(own, HD), cols].astype(F32), axis=0, keepdims=True
        )
        height = jnp.zeros((128, TB), F32)
        for w in range(groups):
            part = pl.ds(w * 128, 128)
            d = e_s[part, :] * (dot(v_s[part, kwin], gt) - delta)
            d_s[part, cols] = d.astype(BF16)
            height = height + d
            width = jnp.sum(d.reshape(16, 8, TB), axis=0)
            for i in range(TB // 128):
                gw_s[i, pl.ds(w * 8, 8), :] = width[:, i * 128 : (i + 1) * 128]
        for i in range(TB // 128):
            lanes = pl.ds(tb * TB + i * 128, 128)
            row_mask, col_mask = token_masks(128, i * 128)
            gh_s[i] = height[:, i * 128 : (i + 1) * 128]
            sum_h = gh_s[i, pl.ds(0, 32, stride=4), :]
            for c in range(1, 4):
                sum_h = sum_h + gh_s[i, pl.ds(c, 32, stride=4), :]
            for k in range(32):
                a_s[pl.ds(STRIDE * (31 - k), STRIDE), lanes] = jnp.where(
                    row_mask, jnp.broadcast_to(sum_h[k : k + 1], (STRIDE, 128)), 0.0
                ).astype(BF16)
            for c in range(4):
                sum_w = (
                    gw_s[i, pl.ds(c, groups, stride=8), :] + gw_s[i, pl.ds(c + 4, groups, stride=8), :]
                )
                for w in range(groups):
                    m = 31 - 4 * w - c
                    a_s[pl.ds(span + STRIDE * m, STRIDE), lanes] = jnp.where(
                        col_mask, jnp.broadcast_to(sum_w[w : w + 1], (STRIDE, 128)), 0.0
                    ).astype(BF16)
        dq = dot(kt_s[pl.ds(rows, HD), :], d_s[:, cols]) * SCALE
        dq = dq + dot(tht_ref[...], a_s[pl.ds(0, span), cols])
        dq = dq + dot(twt_ref[tb], a_s[pl.ds(span, span), cols])
        dq_ref[0, :, cols] = dq.astype(BF16)
        tw_s[pl.ds(tb * STRIDE, span), kwin] += dot(a_s[pl.ds(span, span), cols], qz_s[cols, :])

    ks_s[:, kwin] += dot(d_s[...], qz_s[...])
    vs_s[:, kwin] += dot(p_s[...], gz_s[...])
    th_s[:, kwin] += dot(a_s[pl.ds(0, span), :], qz_s[...])

    @pl.when(n == pl.num_programs(0) - 1)
    def _():
        def heads_added(ref):
            total = ref[:, :128]
            for h in range(1, HEADS):
                first = window_start(h)
                turn = (WIN - (HD * h - first)) % WIN
                total = total + pltpu.roll(ref[:, first : first + WIN], turn, 1)[:, :128]
            return total.astype(BF16)

        def fill(k_out, v_out):
            k_out[:, pl.ds(0, C)] = (ks_s[...] * SCALE).astype(BF16)
            v_out[:, pl.ds(0, C)] = vs_s[...].astype(BF16)
            for out, ref, at in ((k_out, th_s, at_ref[0]), (v_out, tw_s, at_ref[1])):
                out[:, pl.ds(C, 128)] = jnp.zeros((keys, 128), BF16)
                first = pl.multiple_of(STRIDE * at, STRIDE)
                out[pl.ds(first, ref.shape[0]), pl.ds(C, 128)] = heads_added(ref)

        @pl.when(at_ref[2] == 0)
        def _():
            fill(keep_ref, send_ref)

        @pl.when(at_ref[2] == 1)
        def _():
            fill(send_ref, keep_ref)


def attention(at, mine, other, qt, gt, q, g, hexp, wexp, tht, twt):
    tokens = qt.shape[2]
    keys = mine.shape[0]
    span = tht.shape[1]
    whole = lambda shape: pl.BlockSpec(shape, lambda n: (0,) * len(shape))
    head = lambda shape: pl.BlockSpec((1,) + shape, lambda n: (n, 0, 0))
    return pl.pallas_call(
        attention_kernel,
        grid=(HEADS,),
        in_specs=[
            pl.BlockSpec(memory_space=pltpu.SMEM),
            whole(mine.shape),
            whole(other.shape),
            head((WIN, tokens)),
            head((WIN, tokens)),
            whole(q.shape),
            whole(g.shape),
            head((128, tokens)),
            head((64, tokens)),
            whole(tht.shape),
            whole(twt.shape),
        ],
        out_specs=[whole((keys, C + 128)), whole((keys, C + 128)), head((HD, tokens))],
        out_shape=[
            jax.ShapeDtypeStruct((keys, C + 128), BF16),
            jax.ShapeDtypeStruct((keys, C + 128), BF16),
            jax.ShapeDtypeStruct((HEADS, HD, tokens), BF16),
        ],
        scratch_shapes=[
            pltpu.VMEM((keys, C), BF16),
            pltpu.VMEM((keys, C), BF16),
            pltpu.VMEM((C, keys), BF16),
            pltpu.VMEM((C, keys), BF16),
            pltpu.VMEM((keys, TB), F32),
            pltpu.VMEM((keys, tokens), BF16),
            pltpu.VMEM((keys, tokens), BF16),
            pltpu.VMEM((keys, C), F32),
            pltpu.VMEM((keys, C), F32),
            pltpu.VMEM((TB // 128, 128, 128), F32),
            pltpu.VMEM((TB // 128, 64, 128), F32),
            pltpu.VMEM((2 * span, tokens), BF16),
            pltpu.VMEM((tokens, WIN), BF16),
            pltpu.VMEM((tokens, WIN), BF16),
            pltpu.VMEM((span, C), F32),
            pltpu.VMEM((span + STRIDE * (tokens // TB - 1), C), F32),
        ],
        compiler_params=pltpu.CompilerParams(
            dimension_semantics=("arbitrary",), vmem_limit_bytes=60 * 1024 * 1024
        ),
        cost_estimate=pl.CostEstimate(
            flops=16 * keys * tokens * C, bytes_accessed=12 * 1024 * 1024,
            transcendentals=keys * tokens * HEADS,
        ),
        name="attention",
    )(at, mine, other, qt, gt, q, g, hexp, wexp, tht, twt)


def on_device(
    queries, key_tokens, value_tokens, out_grad, key_kernel, value_kernel, height_table, width_table
):
    own_rows, own_cols, _ = queries.shape
    rows_n, cols_n = lax.axis_size("ha"), lax.axis_size("wa")
    tokens = own_rows * own_cols
    cells = own_cols // STRIDE
    ha, wa = lax.axis_index("ha"), lax.axis_index("wa")
    span = STRIDE * rows_n

    part = jnp.stack([pool_partial(key_tokens, key_kernel), pool_partial(value_tokens, value_kernel)])
    left = shift(part[:, :, cells], "wa", 1)
    part = jnp.concatenate([part[:, :, :1] + left[:, :, None], part[:, :, 1:cells]], 2)
    own = part[:, 0] + shift(part[:, 1], "ha", 1)
    pooled = own.astype(BF16)
    pooled, queries, out_grad, height_table, width_table = lax.optimization_barrier(
        (pooled, queries, out_grad, height_table, width_table)
    )
    mine = jnp.broadcast_to(pooled[None], (rows_n // 2, 2, cells, C)).reshape(rows_n, cells, C)
    mine = exchange(mine, "ha").reshape(rows_n * cells, C)
    mine = to_all(mine, "wa").reshape(cols_n * rows_n * cells, C)

    th = lax.dynamic_slice_in_dim(height_table, own_rows * ha, span, 0)
    tw = lax.dynamic_slice_in_dim(width_table, own_cols * wa, span + STRIDE * (cells - 1), 0)
    tht = th.T
    twt = jnp.stack([tw[STRIDE * a : STRIDE * a + span].T for a in range(cells)])
    qt, gt, hexp, wexp = prepare(queries, out_grad, th, tw)
    mine, tht, twt, qt, gt, hexp, wexp = lax.optimization_barrier(
        (mine, tht, twt, qt, gt, hexp, wexp)
    )
    other = swap(mine)

    at = jnp.stack([ha, wa * cells, ha % 2]).astype(jnp.int32)
    keep, send, dq = attention(
        at, mine, other, qt, gt, queries, out_grad, hexp, wexp, tht, twt
    )

    sums = (keep.astype(F32) + swap(send).astype(F32)).astype(BF16)
    sums = exchange(sums.reshape(cols_n, rows_n * cells, C + 128), "wa")
    sums = jnp.sum(sums.astype(F32), 0).astype(BF16)
    half = rows_n * cells // 2
    table = sums[:, C : C + HD].reshape(1, 2, cells, half // cells * HD)
    table = jnp.broadcast_to(table, (rows_n // 2,) + table.shape[1:])
    sums = jnp.concatenate(
        [sums[:, :C].reshape(rows_n, cells, C), table.reshape(rows_n, cells, half // cells * HD)], 2
    )
    sums = exchange(sums, "ha")
    sums = jnp.sum(sums.reshape(rows_n // 2, 2, cells, -1).astype(F32), 0)
    table = sums[:, :, C:].astype(BF16).reshape(2, half, HD)
    table = jnp.pad(table, ((0, 0), (0, 0), (0, 128 - HD)))
    table = to_all(jnp.concatenate([table[0], table[1]], 1), "wa")
    far = swap(table)
    table = jnp.stack([jnp.where(ha % 2 == 0, table, far), jnp.where(ha % 2 == 0, far, table)], 1)
    table = table.reshape(2 * span, 256)
    height_grad = table[: height_table.shape[0], :HD].astype(F32)
    width_grad = table[: width_table.shape[0], 128 : 128 + HD].astype(F32)
    sums = sums[:, :, :C]

    right = shift(sums[:, :1], "wa", -1)
    below = shift(sums, "ha", -1)
    corner = shift_both(sums[:, :1], -1)
    cot = jnp.stack(
        [jnp.concatenate([sums, right], 1), jnp.concatenate([below, corner], 1)], 1
    )
    key_grad = spread(cot[0], key_kernel)
    value_grad = spread(cot[1], value_kernel)

    query_grad = dq.reshape(C, cells, own_rows, STRIDE).transpose(2, 1, 3, 0)
    query_grad = query_grad.reshape(own_rows, own_cols, C)
    return (query_grad, key_grad, value_grad, height_grad, width_grad)


def solution(mesh):
    placed = P("ha", "wa", None)
    return jax.shard_map(
        on_device,
        mesh=mesh,
        in_specs=(placed,) * 4 + (P(),) * 4,
        out_specs=(placed, placed, placed, P(), P()),
        check_vma=False,
    )
```

```python
import math

import jax
import jax.numpy as jnp
from jax import lax
from jax.experimental import pallas as pl
from jax.experimental.pallas import tpu as pltpu
from jax.sharding import PartitionSpec as P


HEADS = 4
HD = 96
C = HEADS * HD
STRIDE = 16
F32 = jnp.float32
BF16 = jnp.bfloat16
SCALE = HD ** (-0.5)
ROOT = HD ** 0.5
EXPONENT = SCALE / math.log(2.0)
WIN = 256
TB = 256


def window_start(n):
    return 128 * (n // 2)


def pool_kernel(k0, k1, k15, v0, v1, v15, kk_ref, vk_ref, own_ref, down_ref, right_ref, corner_ref):
    cells = own_ref.shape[1]
    for t, (rows, kernel) in enumerate((((k0, k1, k15), kk_ref), ((v0, v1, v15), vk_ref))):
        weight = [kernel[i].astype(F32) for i in range(3)]
        tap = lambda i, j: weight[i][j : j + 1]
        own, down = [0.0] * (cells + 1), [0.0] * (cells + 1)
        for c in range(cells):
            top, second, last = [
                x[0, pl.ds(STRIDE * c, STRIDE), :].astype(F32) for x in rows
            ]
            for i, x, to in ((1, top, own), (2, second, own), (0, last, down)):
                to[c] = to[c] + (x[0:1] * tap(i, 1) + x[1:2] * tap(i, 2))
                to[c + 1] = to[c + 1] + x[STRIDE - 1 : STRIDE] * tap(i, 0)
        for c in range(cells):
            own_ref[t, pl.ds(c, 1), :] = own[c]
            down_ref[t, pl.ds(c, 1), :] = down[c]
        right_ref[t] = own[cells]
        corner_ref[t] = down[cells]


def pool_partial(key_tokens, value_tokens, key_kernel, value_kernel):
    _, cols, _ = key_tokens.shape
    cells = cols // STRIDE
    row = lambda r: pl.BlockSpec((1, cols, C), lambda i, r=r: (r, 0, 0))
    whole = lambda shape: pl.BlockSpec(shape, lambda i: (0,) * len(shape))
    rows = [row(0), row(1), row(STRIDE - 1)]
    shapes = [(2, cells, C), (2, cells, C), (2, 1, C), (2, 1, C)]
    return pl.pallas_call(
        pool_kernel,
        grid=(1,),
        in_specs=rows + rows + [whole(key_kernel.shape), whole(value_kernel.shape)],
        out_specs=[whole(x) for x in shapes],
        out_shape=[jax.ShapeDtypeStruct(x, F32) for x in shapes],
        name="pool",
    )(*(key_tokens,) * 3, *(value_tokens,) * 3, key_kernel, value_kernel)


def pooled_kernel(own_ref, above_ref, left_ref, corner_ref, out_ref):
    for t in range(2):
        full = own_ref[t] + above_ref[t]
        first = full[0:1] + (left_ref[t] + corner_ref[t])
        at = lax.broadcasted_iota(jnp.int32, full.shape, 0)
        full = jnp.where(at == 0, jnp.broadcast_to(first, full.shape), full).astype(BF16)
        for i in range(out_ref.shape[0] // 2):
            out_ref[2 * i + t] = full


def pooled_copies(own, above, left, corner, copies):
    whole = pl.BlockSpec(memory_space=pltpu.VMEM)
    return pl.pallas_call(
        pooled_kernel,
        in_specs=[whole] * 4,
        out_specs=whole,
        out_shape=jax.ShapeDtypeStruct((copies,) + own.shape[1:], BF16),
        name="pooled",
    )(own, above, left, corner)


def spread_kernel(
    sums_ref, right_ref, below_ref, corner_ref, kk_ref, vk_ref, key_out_ref, value_out_ref
):
    cells = sums_ref.shape[1]
    at = lax.broadcasted_iota(jnp.int32, (STRIDE, C), 0)
    wide = lambda x: jnp.broadcast_to(x, (STRIDE, C))
    for t, (kernel, out) in enumerate(((kk_ref, key_out_ref), (vk_ref, value_out_ref))):
        weight = [kernel[i].astype(F32) for i in range(3)]
        tap = lambda i, j: weight[i][j : j + 1]
        own, low = sums_ref[t], below_ref[t]
        near = [own[c : c + 1] for c in range(cells)] + [right_ref[t]]
        far = [low[c : c + 1] for c in range(cells)] + [corner_ref[t]]
        out[...] = jnp.zeros_like(out)
        for row, i, cell in ((0, 1, near), (1, 2, near), (STRIDE - 1, 0, far)):
            for c in range(cells):
                value = jnp.where(at == 0, wide(cell[c] * tap(i, 1)), 0.0)
                value = jnp.where(at == 1, wide(cell[c] * tap(i, 2)), value)
                value = jnp.where(at == STRIDE - 1, wide(cell[c + 1] * tap(i, 0)), value)
                out[row, pl.ds(STRIDE * c, STRIDE), :] = value.astype(BF16)


def spread(sums, right, below, corner, key_kernel, value_kernel, shape):
    whole = pl.BlockSpec(memory_space=pltpu.VMEM)
    return pl.pallas_call(
        spread_kernel,
        in_specs=[whole] * 6,
        out_specs=[whole] * 2,
        out_shape=[jax.ShapeDtypeStruct(shape, BF16)] * 2,
        name="spread",
    )(sums, right, below, corner, key_kernel, value_kernel)


def shift(block, axis, distance):
    size = lax.axis_size(axis)
    return lax.ppermute(
        block, axis, [(i, i + distance) for i in range(size) if 0 <= i + distance < size]
    )


def shift_both(block, distance):
    rows, cols = lax.axis_size("ha"), lax.axis_size("wa")
    route = [
        (i * cols + j, (i + distance) * cols + j + distance)
        for i in range(rows)
        for j in range(cols)
        if 0 <= i + distance < rows and 0 <= j + distance < cols
    ]
    return lax.ppermute(block, ("ha", "wa"), route)


def swap(block):
    return lax.ppermute(block, "ha", [(i, i ^ 1) for i in range(lax.axis_size("ha"))])


def to_all(block, axis):
    copies = jnp.broadcast_to(block[None], (lax.axis_size(axis),) + block.shape)
    return lax.all_to_all(copies, axis, 0, 0, tiled=False)


def exchange(blocks, axis):
    return lax.all_to_all(blocks, axis, 0, 0, tiled=False)


def dot(a, b):
    return jnp.dot(a, b, preferred_element_type=F32)


def token_masks(width, first):
    at = lax.broadcasted_iota(jnp.int32, (STRIDE, width), 1) + first
    entry = lax.broadcasted_iota(jnp.int32, (STRIDE, width), 0)
    return at // STRIDE == entry, at % STRIDE == entry


def prep_kernel(q_ref, g_ref, th_ref, tw_ref, qt_ref, gt_ref, hexp_ref, wexp_ref):
    jb = pl.program_id(0)
    row_mask, col_mask = token_masks(TB, 0)
    sub = lax.broadcasted_iota(jnp.int32, (8, TB), 0) % 4
    low = lax.broadcasted_iota(jnp.int32, (8, TB), 0) < 4
    qt = q_ref[...].astype(F32).reshape(TB, C).T.astype(BF16)
    gt = g_ref[...].astype(F32).reshape(TB, C).T.astype(BF16)
    shifted = pl.ds(pl.multiple_of(STRIDE * jb, STRIDE), th_ref.shape[0])
    qt_ref[...] = jnp.zeros_like(qt_ref)
    gt_ref[...] = jnp.zeros_like(gt_ref)
    for n in range(HEADS):
        left = HD * n - window_start(n)
        q_n = qt[HD * n : HD * (n + 1)]
        qt_ref[n, pl.ds(left, HD), :] = q_n
        gt_ref[n, pl.ds(left, HD), :] = gt[HD * n : HD * (n + 1)]

        def picked(table, mask):
            full = dot(table, q_n).reshape(-1, STRIDE, TB)
            full = jnp.where(mask[None], full, 0.0)
            return jnp.sum(full, axis=1, keepdims=True) * ROOT

        rel = picked(th_ref[...], row_mask)
        count = rel.shape[0]
        spread_to = lambda x: jnp.broadcast_to(x, (8, TB))
        for r in range(count // 2):
            hexp_ref[n, pl.ds(8 * r, 8), :] = jnp.where(
                low, spread_to(rel[count - 1 - 2 * r]), spread_to(rel[count - 2 - 2 * r])
            )
        rel = picked(tw_ref[shifted, :], col_mask)
        for w in range(count // 4):
            last = count - 1 - 4 * w
            value = spread_to(rel[last])
            for c in range(1, 4):
                value = jnp.where(sub == c, spread_to(rel[last - c]), value)
            wexp_ref[n, pl.ds(8 * w, 8), :] = value


def prepare(queries, out_grad, th, tw):
    rows, cols, _ = queries.shape
    tokens = rows * cols
    block = pl.BlockSpec((rows, STRIDE, C), lambda j: (0, j, 0))
    whole = lambda x: pl.BlockSpec(x.shape, lambda j: (0, 0))
    out = lambda n: pl.BlockSpec((HEADS, n, TB), lambda j: (0, 0, j))
    return pl.pallas_call(
        prep_kernel,
        grid=(tokens // TB,),
        in_specs=[block, block, whole(th), whole(tw)],
        out_specs=[out(WIN), out(WIN), out(128), out(64)],
        out_shape=[
            jax.ShapeDtypeStruct((HEADS, WIN, tokens), BF16),
            jax.ShapeDtypeStruct((HEADS, WIN, tokens), BF16),
            jax.ShapeDtypeStruct((HEADS, 128, tokens), F32),
            jax.ShapeDtypeStruct((HEADS, 64, tokens), F32),
        ],
        cost_estimate=pl.CostEstimate(
            flops=4 * 1024 * tokens * C, bytes_accessed=10 * 1024 * 1024, transcendentals=0
        ),
        name="prepare",
    )(queries, out_grad, th, tw)


def attention_kernel(
    at_ref, mine_ref, other_ref, qt_ref, gt_ref, q_ref, g_ref, hexp_ref, wexp_ref, tht_ref, twt_ref,
    keep_ref, send_ref, dq_ref,
    k_s, v_s, kt_s, vt_s, e_s, p_s, d_s, ks_s, vs_s, gh_s, gw_s, a_s, qz_s, gz_s, th_s, tw_s,
):
    n = pl.program_id(0)
    keys = k_s.shape[0]
    tokens = qt_ref.shape[2]
    groups = keys // 128
    span = tht_ref.shape[1]

    @pl.when(n == 0)
    def _():
        for parity, (k_ref, v_ref) in enumerate(
            ((mine_ref, other_ref), (other_ref, mine_ref))
        ):

            @pl.when(at_ref[2] == parity)
            def _(k_ref=k_ref, v_ref=v_ref):
                k_s[...] = k_ref[...]
                v_s[...] = v_ref[...]

        kt_s[...] = k_s[...].astype(F32).T.astype(BF16)
        vt_s[...] = v_s[...].astype(F32).T.astype(BF16)
        for ref in (ks_s, vs_s, th_s, tw_s):
            ref[...] = jnp.zeros_like(ref)

    win = pl.multiple_of(128 * (n // 2), 128)
    own = pl.multiple_of(HD * n - 128 * (n // 2), 32)
    rows = pl.multiple_of(HD * n, 32)
    kwin = pl.ds(win, WIN)
    lane = lax.broadcasted_iota(jnp.int32, (1, WIN), 1)
    lanes_on = ((lane >= own) & (lane < own + HD)).astype(F32).astype(BF16)

    blocks = tokens // TB
    for tb in range(blocks):
        tile = (slice(None), pl.ds(tb * STRIDE, STRIDE), kwin)
        qz_s[pl.ds(tb * TB, TB), :] = q_ref[tile].reshape(TB, WIN) * lanes_on
        gz_s[pl.ds(tb * TB, TB), :] = g_ref[tile].reshape(TB, WIN) * lanes_on

    def scores(tb, w, top):
        cols, part = pl.ds(tb * TB, TB), pl.ds(w * 128, 128)
        s = dot(k_s[part, kwin], qt_ref[0, :, cols])
        bias = wexp_ref[0, pl.ds(w * 8, 8), cols]
        s = (s + hexp_ref[0, :, cols]).reshape(16, 8, TB) + bias[None]
        e_s[tb % 2, part, :] = s.reshape(128, TB)
        return jnp.maximum(top, jnp.max(s, axis=0))

    lowest = jnp.full((8, TB), -jnp.inf, F32)
    following = lowest
    for w in range(groups):
        following = scores(0, w, following)
    for tb in range(blocks):
        cols = pl.ds(tb * TB, TB)
        top = jnp.max(following, axis=0, keepdims=True)
        following = lowest
        total = jnp.zeros((8, TB), F32)
        for w in range(groups):
            part = pl.ds(w * 128, 128)
            e = jnp.exp2((e_s[tb % 2, part, :] - top) * EXPONENT)
            total = total + jnp.sum(e.reshape(16, 8, TB), axis=0)
            e_s[tb % 2, part, :] = e
            if tb + 1 < blocks:
                following = scores(tb + 1, w, following)
        inverse = 1.0 / jnp.sum(total, axis=0, keepdims=True)
        for w in range(groups):
            part = pl.ds(w * 128, 128)
            p = e_s[tb % 2, part, :] * inverse
            e_s[tb % 2, part, :] = p
            p_s[part, cols] = p.astype(BF16)
        gt = gt_ref[0, :, cols]
        attended = dot(vt_s[pl.ds(rows, HD), :], p_s[:, cols])
        delta = jnp.sum(
            attended * gt_ref[0, pl.ds(own, HD), cols].astype(F32), axis=0, keepdims=True
        )
        height = jnp.zeros((128, TB), F32)
        for w in range(groups):
            part = pl.ds(w * 128, 128)
            d = e_s[tb % 2, part, :] * (dot(v_s[part, kwin], gt) - delta)
            d_s[part, cols] = d.astype(BF16)
            height = height + d
            width = jnp.sum(d.reshape(16, 8, TB), axis=0)
            for i in range(TB // 128):
                gw_s[i, pl.ds(w * 8, 8), :] = width[:, i * 128 : (i + 1) * 128]
        for i in range(TB // 128):
            lanes = pl.ds(tb * TB + i * 128, 128)
            row_mask, col_mask = token_masks(128, i * 128)
            gh_s[i] = height[:, i * 128 : (i + 1) * 128]
            sum_h = gh_s[i, pl.ds(0, 32, stride=4), :]
            for c in range(1, 4):
                sum_h = sum_h + gh_s[i, pl.ds(c, 32, stride=4), :]
            for k in range(32):
                a_s[pl.ds(STRIDE * (31 - k), STRIDE), lanes] = jnp.where(
                    row_mask, jnp.broadcast_to(sum_h[k : k + 1], (STRIDE, 128)), 0.0
                ).astype(BF16)
            for c in range(4):
                sum_w = (
                    gw_s[i, pl.ds(c, groups, stride=8), :] + gw_s[i, pl.ds(c + 4, groups, stride=8), :]
                )
                for w in range(groups):
                    m = 31 - 4 * w - c
                    a_s[pl.ds(span + STRIDE * m, STRIDE), lanes] = jnp.where(
                        col_mask, jnp.broadcast_to(sum_w[w : w + 1], (STRIDE, 128)), 0.0
                    ).astype(BF16)
        dq = dot(kt_s[pl.ds(rows, HD), :], d_s[:, cols]) * SCALE
        dq = dq + dot(tht_ref[...], a_s[pl.ds(0, span), cols])
        dq = dq + dot(twt_ref[tb], a_s[pl.ds(span, span), cols])
        dq_ref[0, :, cols] = dq.astype(BF16)
        tw_s[pl.ds(tb * STRIDE, span), kwin] += dot(a_s[pl.ds(span, span), cols], qz_s[cols, :])

    ks_s[:, kwin] += dot(d_s[...], qz_s[...])
    vs_s[:, kwin] += dot(p_s[...], gz_s[...])
    th_s[:, kwin] += dot(a_s[pl.ds(0, span), :], qz_s[...])

    @pl.when(n == pl.num_programs(0) - 1)
    def _():
        def heads_added(ref):
            total = ref[:, :128]
            for h in range(1, HEADS):
                first = window_start(h)
                turn = (WIN - (HD * h - first)) % WIN
                total = total + pltpu.roll(ref[:, first : first + WIN], turn, 1)[:, :128]
            return total.astype(BF16)

        def fill(k_out, v_out):
            k_out[:, pl.ds(0, C)] = (ks_s[...] * SCALE).astype(BF16)
            v_out[:, pl.ds(0, C)] = vs_s[...].astype(BF16)
            for out, ref, at in ((k_out, th_s, at_ref[0]), (v_out, tw_s, at_ref[1])):
                out[:, pl.ds(C, 128)] = jnp.zeros((keys, 128), BF16)
                first = pl.multiple_of(STRIDE * at, STRIDE)
                out[pl.ds(first, ref.shape[0]), pl.ds(C, 128)] = heads_added(ref)

        @pl.when(at_ref[2] == 0)
        def _():
            fill(keep_ref, send_ref)

        @pl.when(at_ref[2] == 1)
        def _():
            fill(send_ref, keep_ref)


def attention(at, mine, other, qt, gt, q, g, hexp, wexp, tht, twt):
    tokens = qt.shape[2]
    keys = mine.shape[0]
    span = tht.shape[1]
    whole = lambda shape: pl.BlockSpec(shape, lambda n: (0,) * len(shape))
    head = lambda shape: pl.BlockSpec((1,) + shape, lambda n: (n, 0, 0))
    return pl.pallas_call(
        attention_kernel,
        grid=(HEADS,),
        in_specs=[
            pl.BlockSpec(memory_space=pltpu.SMEM),
            whole(mine.shape),
            whole(other.shape),
            head((WIN, tokens)),
            head((WIN, tokens)),
            whole(q.shape),
            whole(g.shape),
            head((128, tokens)),
            head((64, tokens)),
            whole(tht.shape),
            whole(twt.shape),
        ],
        out_specs=[whole((keys, C + 128)), whole((keys, C + 128)), head((HD, tokens))],
        out_shape=[
            jax.ShapeDtypeStruct((keys, C + 128), BF16),
            jax.ShapeDtypeStruct((keys, C + 128), BF16),
            jax.ShapeDtypeStruct((HEADS, HD, tokens), BF16),
        ],
        scratch_shapes=[
            pltpu.VMEM((keys, C), BF16),
            pltpu.VMEM((keys, C), BF16),
            pltpu.VMEM((C, keys), BF16),
            pltpu.VMEM((C, keys), BF16),
            pltpu.VMEM((2, keys, TB), F32),
            pltpu.VMEM((keys, tokens), BF16),
            pltpu.VMEM((keys, tokens), BF16),
            pltpu.VMEM((keys, C), F32),
            pltpu.VMEM((keys, C), F32),
            pltpu.VMEM((TB // 128, 128, 128), F32),
            pltpu.VMEM((TB // 128, 64, 128), F32),
            pltpu.VMEM((2 * span, tokens), BF16),
            pltpu.VMEM((tokens, WIN), BF16),
            pltpu.VMEM((tokens, WIN), BF16),
            pltpu.VMEM((span, C), F32),
            pltpu.VMEM((span + STRIDE * (tokens // TB - 1), C), F32),
        ],
        compiler_params=pltpu.CompilerParams(
            dimension_semantics=("arbitrary",), vmem_limit_bytes=60 * 1024 * 1024
        ),
        cost_estimate=pl.CostEstimate(
            flops=16 * keys * tokens * C, bytes_accessed=12 * 1024 * 1024,
            transcendentals=keys * tokens * HEADS,
        ),
        name="attention",
    )(at, mine, other, qt, gt, q, g, hexp, wexp, tht, twt)


def table_kernel(at_ref, mine_ref, other_ref, height_ref, width_ref):
    blocks, half, _ = mine_ref.shape

    def fill(even, odd):
        for w in range(blocks):
            block = jnp.concatenate([even[w], odd[w]], 0).astype(F32)
            first = 2 * half * w
            count = min(2 * half, height_ref.shape[1] - first)
            for i, out in enumerate((height_ref, width_ref)):
                turned = block[:, 128 * i : 128 * (i + 1)].T
                out[:, first : first + count] = turned[:HD, :count]

    @pl.when(at_ref[2] == 0)
    def _():
        fill(mine_ref, other_ref)

    @pl.when(at_ref[2] == 1)
    def _():
        fill(other_ref, mine_ref)


def tables_out(at, mine, other, entries):
    whole = pl.BlockSpec(memory_space=pltpu.VMEM)
    height, width = pl.pallas_call(
        table_kernel,
        in_specs=[pl.BlockSpec(memory_space=pltpu.SMEM), whole, whole],
        out_specs=[whole, whole],
        out_shape=[jax.ShapeDtypeStruct((HD, entries), F32)] * 2,
        name="tables",
    )(at, mine, other)
    return height.T, width.T


def turn_kernel(dq_ref, out_ref):
    for tb in range(dq_ref.shape[2] // TB):
        block = dq_ref[:, :, pl.ds(tb * TB, TB)].reshape(C, TB).astype(F32).T.astype(BF16)
        out_ref[:, pl.ds(tb * STRIDE, STRIDE), :] = block.reshape(-1, STRIDE, C)


def turn(dq, shape):
    whole = pl.BlockSpec(memory_space=pltpu.VMEM)
    return pl.pallas_call(
        turn_kernel,
        in_specs=[whole],
        out_specs=whole,
        out_shape=jax.ShapeDtypeStruct(shape, BF16),
        name="turn",
    )(dq)


def on_device(
    queries, key_tokens, value_tokens, out_grad, key_kernel, value_kernel, height_table, width_table
):
    own_rows, own_cols, _ = queries.shape
    rows_n, cols_n = lax.axis_size("ha"), lax.axis_size("wa")
    cells = own_cols // STRIDE
    ha, wa = lax.axis_index("ha"), lax.axis_index("wa")
    span = STRIDE * rows_n

    own, down, right, corner = pool_partial(key_tokens, value_tokens, key_kernel, value_kernel)
    corner = shift_both(corner, 1)
    above = shift(down, "ha", 1)
    left = shift(right, "wa", 1)
    mine = pooled_copies(own, above, left, corner, rows_n)
    mine, queries, out_grad, height_table, width_table = lax.optimization_barrier(
        (mine, queries, out_grad, height_table, width_table)
    )
    mine = exchange(mine, "ha").reshape(rows_n * cells, C)
    mine = to_all(mine, "wa").reshape(cols_n * rows_n * cells, C)

    th = lax.dynamic_slice_in_dim(height_table, own_rows * ha, span, 0)
    tw = lax.dynamic_slice_in_dim(width_table, own_cols * wa, span + STRIDE * (cells - 1), 0)
    tht = th.T
    twt = jnp.stack([tw[STRIDE * a : STRIDE * a + span].T for a in range(cells)])
    qt, gt, hexp, wexp = prepare(queries, out_grad, th, tw)
    mine, tht, twt, qt, gt, hexp, wexp = lax.optimization_barrier(
        (mine, tht, twt, qt, gt, hexp, wexp)
    )
    other = swap(mine)

    at = jnp.stack([ha, wa * cells, ha % 2]).astype(jnp.int32)
    keep, send, dq = attention(
        at, mine, other, qt, gt, queries, out_grad, hexp, wexp, tht, twt
    )

    sums = (keep.astype(F32) + swap(send).astype(F32)).astype(BF16)
    sums = exchange(sums.reshape(cols_n, rows_n * cells, C + 128), "wa")
    sums = jnp.sum(sums.astype(F32), 0).astype(BF16)
    half = rows_n * cells // 2
    table = sums[:, C : C + HD].reshape(1, 2, cells, half // cells * HD)
    table = jnp.broadcast_to(table, (rows_n // 2,) + table.shape[1:])
    sums = jnp.concatenate(
        [sums[:, :C].reshape(rows_n, cells, C), table.reshape(rows_n, cells, half // cells * HD)], 2
    )
    sums = exchange(sums, "ha")
    sums = jnp.sum(sums.reshape(rows_n // 2, 2, cells, -1).astype(F32), 0)
    table = sums[:, :, C:].astype(BF16).reshape(2, half, HD)
    table = jnp.pad(table, ((0, 0), (0, 0), (0, 128 - HD)))
    table = to_all(jnp.concatenate([table[0], table[1]], 1), "wa")
    height_grad, width_grad = tables_out(at, table, swap(table), height_table.shape[0])
    sums = sums[:, :, :C]

    corner = shift_both(sums[:, :1], -1)
    below = shift(sums, "ha", -1)
    right = shift(sums[:, :1], "wa", -1)
    key_grad, value_grad = spread(
        sums, right, below, corner, key_kernel, value_kernel, key_tokens.shape
    )

    query_grad = turn(dq, queries.shape)
    return (query_grad, key_grad, value_grad, height_grad, width_grad)


def solution(mesh):
    placed = P("ha", "wa", None)
    return jax.shard_map(
        on_device,
        mesh=mesh,
        in_specs=(placed,) * 4 + (P(),) * 4,
        out_specs=(placed, placed, placed, P(), P()),
        check_vma=False,
    )
```
